32 devices in a mesh: batch: 8 (over y, x, core), tile: 4 (over z).
Axes of the slice: x: 2, y: 2, z: 4, core: 2. Of those that a mesh axis runs over, the one named last changes fastest.
Arguments:
- object_field: float32 [2, 2, 3072, 1536], P(None, None, 'batch', 'tile'), may hold values from -6 to 6
- probe_wave: bfloat16 [2, 256, 256], replicated, may hold values from -4.1875 to 4.1875
- intensities: float32 [512, 256, 256], P(('batch', 'tile')), may hold values from 0 to 4
- owner_rows: int32 [512, 1], P(('batch', 'tile')), may hold values from 0 to 7; in each aligned block of 16 rows (0 to 15, 16 to 31, ...) at most 4 rows name the same one
- offsets: int32 [512, 2], P(('batch', 'tile')), may hold values from 0 to 128
Outputs:
- new_object: float32 [2, 2, 3072, 1536], P(None, None, 'batch', 'tile')
- new_probe: float32 [2, 256, 256], replicated
The draws below stay inside these ranges and needn't reach their ends.
Inputs may be any that keep to these rules, and one draw needn't show every extreme that they name: `owner_rows`: within the 16 positions of one device, each tile row is named at most 4 times.
All inputs are finite; a program needn't handle non-finite values.
Results may differ from the reference program's by a relative error of at most 0.008.
The reference program's roundings to bfloat16 on the way count: a program that leaves them out, or rounds other values in their place, can miss the bound.
Values may be sent and summed in bfloat16 or wider, within the bound.
A program may use at most 192 MiB of HBM per device.

```python
import math
import jax
import jax.numpy as jnp
import numpy as np
from jax import lax

W = 256
S = 2
TS = 384
P_DEV = 16
CAP = 4
POSITIONS = 512
NY = 3072
NX = 1536
N_BATCH = 8
N_TILE = 4


def set_ends(result, rng, least, largest):
    spot = [jax.random.randint(jax.random.fold_in(rng, axis), (), 0, length) for axis, length in enumerate(result.shape)]
    main_axis = result.shape.index(max(result.shape))
    neighbour = spot[:main_axis] + [(spot[main_axis] + 1) % result.shape[main_axis]] + spot[main_axis + 1:]
    return result.at[tuple(spot)].set(least).at[tuple(neighbour)].set(largest)


def shard_levels(rng, dims, cuts, least, top_value):
    def one(dim, shards_of):
        draws = jax.random.uniform(jax.random.fold_in(jax.random.fold_in(rng, 6), dim), (shards_of,), jnp.float32, least / len(cuts), top_value / len(cuts))
        return jnp.repeat(jnp.exp(draws), dims[dim] // shards_of).reshape((-1,) + (1,) * (len(dims) - dim - 1))

    level = one(*cuts[0])
    for cut in cuts[1:]:
        level = level * one(*cut)
    return level


def assign_block(own_key, own, number, rows, count, top, limit, skew):
    sequence = jax.random.permutation(own_key, count)
    packed, usual = load_shares(count, rows * top, limit, skew, True), load_shares(count, rows * top, limit, skew, False)
    places = jnp.arange(count)

    def named(lengths, rotation):
        used = int((lengths > 0).sum())
        fixed = max(1, used // 4)
        shifted = fixed + (places - fixed + rotation * (used - fixed)) % max(1, count - fixed)
        return jnp.zeros((count,), jnp.int32).at[sequence[jnp.where(places < fixed, places, shifted)]].set(jnp.asarray(lengths, jnp.int32))

    lengths = jnp.where(number % 4 == 0, named(packed, number // 4), named(usual, number - number // 4 - 1))
    mixed = jax.random.permutation(jax.random.fold_in(own, 3), count)
    giver, sink = mixed[0:count // 2 * 2:2], mixed[1:count // 2 * 2:2]
    room = jnp.minimum(lengths[giver] - 1, limit - lengths[sink]) // 2
    room = jnp.where((giver == sequence[0]) | (sink == sequence[0]) | (lengths[sink] == 0), 0, jnp.maximum(room, 0))
    shifted = jax.random.randint(jax.random.fold_in(own, 4), (count // 2,), 0, 1 << 20) % (room + 1)
    lengths = lengths.at[giver].add(-shifted).at[sink].add(shifted)
    members = jnp.searchsorted(jnp.cumsum(lengths), jnp.arange(rows * top), side="right").astype(jnp.int32)
    grid = members.reshape(top, rows).T
    grid = grid[jax.random.permutation(jax.random.fold_in(own, 1), rows)]
    rotation = jax.random.randint(jax.random.fold_in(own, 2), (rows, 1), 0, top)
    return jnp.take_along_axis(grid, (jnp.arange(top)[None, :] + rotation) % top, axis=1)


def load_shares(number_of, total, bound, slope, full):
    portions = [(1 << 20) // math.isqrt(standing ** slope) + 1 for standing in range(1, number_of + 1)]
    largest = bound if full else min(bound, max(-(-total // number_of), total * portions[0] // sum(portions)))
    least = 1 if total - largest >= number_of - 1 else 0
    given, spare = [largest] + [least] * (number_of - 1), total - largest - least * (number_of - 1)
    while spare > 0:
        free = [i for i in range(1, number_of) if given[i] < largest] or [i for i in range(1, number_of) if given[i] < bound]
        pool, remaining = sum([portions[i] for i in free]), spare
        for i in free:
            addition = min(bound - given[i], max(1, remaining * portions[i] // pool), spare)
            given[i] = given[i] + addition
            spare = spare - addition
    return np.array(given)


def normal_values(key, dims, scale, reach, cuts=(), held_as=jnp.bfloat16):
    drawn = jax.random.normal(key, dims, jnp.float32) * scale
    if len(cuts) > 0:
        drawn = shard_levels(key, dims, cuts, -0.22, 0.18) * drawn
    return jnp.clip(drawn, min=-reach, max=reach).astype(held_as)


def setup_inputs(seed: int = 0) -> dict:
    streams_of = jax.random.split(jax.random.key(seed), 6)
    object_field = normal_values(streams_of[0], (S, 2, NY, NX), 1.0, 6.0, ((2, 8), (3, 4)), jnp.float32)
    probe_wave = normal_values(streams_of[1], (2, W, W), 0.7, 4.1875)
    intensities = jnp.clip(4.0 * jax.random.uniform(streams_of[2], (POSITIONS, W, W), jnp.float32) ** shard_levels(streams_of[2], (POSITIONS, W, W), ((0, 32),), -0.2, 0.2), 0.0, 4.0)
    owner_rows_keys = jax.random.split(jax.random.fold_in(streams_of[3], 1), POSITIONS // P_DEV)
    owner_rows_turns = jax.random.permutation(jax.random.fold_in(streams_of[3], 3), POSITIONS // P_DEV)
    owner_rows = jax.vmap(lambda own, number: assign_block(jax.random.fold_in(streams_of[3], 2), own, number, P_DEV, N_BATCH, 1, CAP, 2))(owner_rows_keys, owner_rows_turns).reshape((POSITIONS, 1))
    offsets = set_ends(jax.random.randint(streams_of[4], (POSITIONS, 2), 0, TS - W + 1), jax.random.fold_in(streams_of[4], 1), 0, TS - W).astype(jnp.int32)
    return {"object_field": object_field, "probe_wave": probe_wave, "intensities": intensities, "owner_rows": owner_rows, "offsets": offsets}


update_rate = 0.1
tv_weight = 12.0
tv_smooth = 1.0
probe_rate = 0.04

def tables(extent):
    counter = jnp.arange(extent, dtype=jnp.int32)
    product = counter[:, None] * counter[None, :] % extent
    angles = product.astype(jnp.float32) * (2.0 * math.pi / extent)
    scaling = 1.0 / math.sqrt(extent)
    cos_table = (jnp.cos(angles) * scaling).astype(jnp.bfloat16)
    sin_table = (-jnp.sin(angles) * scaling).astype(jnp.bfloat16)
    frequency = (counter + extent // 2) % extent - extent // 2
    squared = (frequency * frequency).astype(jnp.float32)
    phases = -(0.5 / extent) * (squared[:, None] + squared[None, :])
    return (cos_table, sin_table, jnp.cos(phases), jnp.sin(phases))

def transform(real_part, imag_part, cos_table, sin_table):
    extent = real_part.shape[0]
    left_stack = jnp.concatenate([cos_table, sin_table], 0)
    right_stack = jnp.concatenate([real_part, imag_part], 1)
    blocks = jnp.dot(left_stack, right_stack, preferred_element_type=jnp.float32)
    mid_real = (blocks[:extent, :extent] - blocks[extent:, extent:]).astype(jnp.bfloat16)
    mid_imag = (blocks[:extent, extent:] + blocks[extent:, :extent]).astype(jnp.bfloat16)
    left_two = jnp.concatenate([mid_real, mid_imag], 0)
    right_two = jnp.concatenate([cos_table, sin_table], 1)
    second = jnp.dot(left_two, right_two, preferred_element_type=jnp.float32)
    out_real = second[:extent, :extent] - second[extent:, extent:]
    out_imag = second[:extent, extent:] + second[extent:, :extent]
    return (out_real, out_imag)

def multislice(object_patch, probe_wave, measured, cos_table, sin_table, prop_real, prop_imag):
    slices = object_patch.shape[0]
    back_sin = -sin_table
    psi_real = probe_wave[0]
    psi_imag = probe_wave[1]
    entering = []
    for slab_index in range(slices):
        trans_real = object_patch[slab_index, 0].astype(jnp.float32)
        trans_imag = object_patch[slab_index, 1].astype(jnp.float32)
        entering.append((psi_real, psi_imag))
        wave_real = psi_real.astype(jnp.float32)
        wave_imag = psi_imag.astype(jnp.float32)
        prod_real = (wave_real * trans_real - wave_imag * trans_imag).astype(jnp.bfloat16)
        prod_imag = (wave_real * trans_imag + wave_imag * trans_real).astype(jnp.bfloat16)
        if slab_index + 1 < slices:
            far_real, far_imag = transform(prod_real, prod_imag, cos_table, sin_table)
            kick_real = (prop_real * far_real - prop_imag * far_imag).astype(jnp.bfloat16)
            kick_imag = (prop_real * far_imag + prop_imag * far_real).astype(jnp.bfloat16)
            near_real, near_imag = transform(kick_real, kick_imag, cos_table, back_sin)
            psi_real = near_real.astype(jnp.bfloat16)
            psi_imag = near_imag.astype(jnp.bfloat16)
    exit_real, exit_imag = transform(prod_real, prod_imag, cos_table, sin_table)
    misfit = 0.5 * (exit_real * exit_real + exit_imag * exit_imag - measured)
    chi_real = (misfit * exit_real).astype(jnp.bfloat16)
    chi_imag = (misfit * exit_imag).astype(jnp.bfloat16)
    grad_real, grad_imag = transform(chi_real, chi_imag, cos_table, back_sin)
    object_grads = [None] * slices
    for slab_index in reversed(range(slices)):
        trans_real = object_patch[slab_index, 0].astype(jnp.float32)
        trans_imag = object_patch[slab_index, 1].astype(jnp.float32)
        wave_real = entering[slab_index][0].astype(jnp.float32)
        wave_imag = entering[slab_index][1].astype(jnp.float32)
        object_grads[slab_index] = jnp.stack([grad_real * wave_real + grad_imag * wave_imag, grad_imag * wave_real - grad_real * wave_imag])
        dpsi_real = grad_real * trans_real + grad_imag * trans_imag
        dpsi_imag = grad_imag * trans_real - grad_real * trans_imag
        if slab_index > 0:
            back_real, back_imag = transform(dpsi_real.astype(jnp.bfloat16), dpsi_imag.astype(jnp.bfloat16), cos_table, back_sin)
            turn_real = (prop_real * back_real + prop_imag * back_imag).astype(jnp.bfloat16)
            turn_imag = (prop_real * back_imag - prop_imag * back_real).astype(jnp.bfloat16)
            grad_real, grad_imag = transform(turn_real, turn_imag, cos_table, sin_table)
    patch_grad = jnp.stack(object_grads).astype(jnp.bfloat16)
    probe_grad = jnp.stack([dpsi_real, dpsi_imag])
    return (patch_grad, probe_grad)

def tv_gradient(field):
    down_diff = jnp.roll(field, -1, axis=2) - field
    right_diff = jnp.roll(field, -1, axis=3) - field
    weight = 1.0 / jnp.sqrt(lax.optimization_barrier(jnp.sum(down_diff * down_diff + right_diff * right_diff, axis=1, keepdims=True)) + tv_smooth)
    flow_down = weight * down_diff
    flow_right = weight * right_diff
    return jnp.roll(flow_down, 1, axis=2) + jnp.roll(flow_right, 1, axis=3) - flow_down - flow_right

def reference(object_field, probe_wave, intensities, owner_rows, offsets):
    cos_table, sin_table, prop_real, prop_imag = tables(W)
    total_rows = intensities.shape[0]
    serial = jnp.arange(total_rows, dtype=jnp.int32)
    columns = serial // P_DEV % N_TILE
    row_start = (owner_rows[:, 0] * TS + offsets[:, 0]).astype(jnp.int32)
    col_start = (columns * TS + offsets[:, 1]).astype(jnp.int32)
    anchor = jnp.zeros((), jnp.int32)

    def visit_one(state_in, inputs):
        field_grad, probe_total = state_in
        measured, row_at, col_at = inputs
        start = (anchor, anchor, row_at, col_at)
        object_patch = lax.dynamic_slice(object_field, start, (S, 2, W, W)).astype(jnp.bfloat16)
        patch_grad, probe_grad = multislice(object_patch, probe_wave, measured, cos_table, sin_table, prop_real, prop_imag)
        current = lax.dynamic_slice(field_grad, start, (S, 2, W, W))
        field_grad = lax.dynamic_update_slice(field_grad, current + patch_grad.astype(jnp.float32), start)
        return ((field_grad, probe_total + probe_grad), None)
    initial = (jnp.zeros(object_field.shape, jnp.float32), jnp.zeros((2, W, W), jnp.float32))
    (field_grad, probe_total), _ = lax.scan(visit_one, initial, (intensities, row_start, col_start))
    new_object = object_field - update_rate * (field_grad + tv_weight * tv_gradient(object_field))
    new_probe = probe_wave.astype(jnp.float32) - probe_rate * probe_total
    return (new_object, new_probe)
```

```python
import math

import jax
import jax.numpy as jnp
from jax import lax
from jax.experimental import pallas as pl
from jax.experimental.pallas import tpu as pltpu
from jax.sharding import PartitionSpec as P

update_rate = 0.1
tv_weight = 12.0
tv_smooth = 1.0
probe_rate = 0.04
sublanes = 8


def extended(x, sides, width):
    for axis, dim in sides:
        size, length = (lax.axis_size(axis), x.shape[dim])
        up = [(i, (i + 1) % size) for i in range(size)]
        down = [(j, i) for i, j in up]
        last = lax.slice_in_dim(x, length - width, length, axis=dim)
        first = lax.slice_in_dim(x, 0, width, axis=dim)
        before = lax.ppermute(last, axis, up)
        after = lax.ppermute(first, axis, down)
        x = jnp.concatenate([before, x, after], axis=dim)
    return x


def tables(extent):
    counter = jnp.arange(extent, dtype=jnp.int32)
    product = counter[:, None] * counter[None, :] % extent
    angles = product.astype(jnp.float32) * (2.0 * math.pi / extent)
    scaling = 1.0 / math.sqrt(extent)
    cos_table = (jnp.cos(angles) * scaling).astype(jnp.bfloat16)
    sin_table = (-jnp.sin(angles) * scaling).astype(jnp.bfloat16)
    frequency = (counter + extent // 2) % extent - extent // 2
    squared = (frequency * frequency).astype(jnp.float32)
    phases = -(0.5 / extent) * (squared[:, None] + squared[None, :])
    return (cos_table, sin_table, jnp.cos(phases), jnp.sin(phases))


def transform(real_part, imag_part, left_table, right_table):
    extent = real_part.shape[0]
    stacked = jnp.concatenate([real_part, imag_part], 0)
    mid = jnp.dot(left_table, stacked, preferred_element_type=jnp.float32).astype(jnp.bfloat16)
    second = jnp.dot(
        jnp.concatenate([mid[:extent], mid[extent:]], 1),
        right_table,
        preferred_element_type=jnp.float32,
    )
    return (second[:, :extent], second[:, extent:])


def visit_kernel(
    plan_ref,
    tile_ref,
    measured_ref,
    probe_ref,
    fore_ref,
    back_ref,
    prop_ref,
    sums_ref,
    total_ref,
    wide,
    summed,
    trans,
    psi,
    total,
):
    step = pl.program_id(0)
    slices = tile_ref.shape[1]
    tile_cols = tile_ref.shape[-1]
    extent = probe_ref.shape[-1]
    last_step = pl.num_programs(0) - 1
    opens = plan_ref[1, step] == 0

    @pl.when(step == 0)
    def _():
        total[...] = jnp.zeros_like(total)

    @pl.when(opens)
    def _():
        wide[:, :, : tile_ref.shape[3], :] = tile_ref[0].astype(jnp.float32)
        summed[...] = jnp.zeros_like(summed)

    @pl.when(jnp.logical_not(opens))
    def _():
        row_at = plan_ref[3, step]
        col_at = plan_ref[4, step]
        back_shift = lax.rem(tile_cols - col_at, tile_cols)
        span = extent + sublanes
        row_rest = lax.rem(row_at, sublanes)
        rows = pl.ds(pl.multiple_of(row_at - row_rest, sublanes), span)
        row_shift = lax.rem(span - row_rest, span)
        fore = fore_ref[...]
        back = back_ref[...]

        def add_grad(slab, part, value):
            value = value.astype(jnp.bfloat16).astype(jnp.float32)
            below = jnp.zeros((sublanes, extent), jnp.float32)
            beside = jnp.zeros((span, tile_cols - extent), jnp.float32)
            value = pltpu.roll(jnp.concatenate([value, below], 0), row_rest, 0)
            placed = pltpu.roll(jnp.concatenate([value, beside], 1), col_at, 1)
            summed[slab, part, rows, :] = summed[slab, part, rows, :] + placed

        for slab in range(slices):
            for part in range(2):
                cut = pltpu.roll(wide[slab, part, rows, :], back_shift, 1)[:, :extent]
                trans[slab, part] = pltpu.roll(cut, row_shift, 0)[:extent]
        psi[0] = probe_ref[...]
        for slab in range(slices):
            wave_real = psi[slab, 0].astype(jnp.float32)
            wave_imag = psi[slab, 1].astype(jnp.float32)
            trans_real = trans[slab, 0]
            trans_imag = trans[slab, 1]
            prod_real = (wave_real * trans_real - wave_imag * trans_imag).astype(jnp.bfloat16)
            prod_imag = (wave_real * trans_imag + wave_imag * trans_real).astype(jnp.bfloat16)
            far_real, far_imag = transform(prod_real, prod_imag, fore, back)
            if slab + 1 < slices:
                prop_real = prop_ref[0]
                prop_imag = prop_ref[1]
                kick_real = (prop_real * far_real - prop_imag * far_imag).astype(jnp.bfloat16)
                kick_imag = (prop_real * far_imag + prop_imag * far_real).astype(jnp.bfloat16)
                near_real, near_imag = transform(kick_real, kick_imag, back, fore)
                psi[slab + 1, 0] = near_real.astype(jnp.bfloat16)
                psi[slab + 1, 1] = near_imag.astype(jnp.bfloat16)
        misfit = 0.5 * (far_real * far_real + far_imag * far_imag - measured_ref[0])
        chi_real = (misfit * far_real).astype(jnp.bfloat16)
        chi_imag = (misfit * far_imag).astype(jnp.bfloat16)
        grad_real, grad_imag = transform(chi_real, chi_imag, back, fore)
        for slab in reversed(range(slices)):
            wave_real = psi[slab, 0].astype(jnp.float32)
            wave_imag = psi[slab, 1].astype(jnp.float32)
            trans_real = trans[slab, 0]
            trans_imag = trans[slab, 1]
            add_grad(slab, 0, grad_real * wave_real + grad_imag * wave_imag)
            add_grad(slab, 1, grad_imag * wave_real - grad_real * wave_imag)
            dpsi_real = grad_real * trans_real + grad_imag * trans_imag
            dpsi_imag = grad_imag * trans_real - grad_real * trans_imag
            if slab > 0:
                back_real, back_imag = transform(
                    dpsi_real.astype(jnp.bfloat16), dpsi_imag.astype(jnp.bfloat16), back, fore
                )
                prop_real = prop_ref[0]
                prop_imag = prop_ref[1]
                turn_real = (prop_real * back_real + prop_imag * back_imag).astype(jnp.bfloat16)
                turn_imag = (prop_real * back_imag - prop_imag * back_real).astype(jnp.bfloat16)
                grad_real, grad_imag = transform(turn_real, turn_imag, fore, back)
        total[0] = total[0] + dpsi_real
        total[1] = total[1] + dpsi_imag

    @pl.when(plan_ref[0, step + 1] != plan_ref[0, step])
    def _():
        sums_ref[0] = summed[:, :, : sums_ref.shape[3], :].astype(jnp.bfloat16)

    @pl.when(step == last_step)
    def _():
        total_ref[...] = total[...]


def visiting_plan(targets, offsets, nbatch):
    local_rows = targets.shape[0]
    steps = local_rows + nbatch
    serial = jnp.arange(local_rows, dtype=jnp.int32)
    ahead = (targets[None, :] < targets[:, None]) | (
        (targets[None, :] == targets[:, None]) & (serial[None, :] < serial[:, None])
    )
    rank = jnp.sum(ahead.astype(jnp.int32), axis=1)
    rows = jnp.arange(nbatch, dtype=jnp.int32)
    opening = rows + jnp.sum((targets[None, :] < rows[:, None]).astype(jnp.int32), axis=1)
    count = jnp.arange(steps, dtype=jnp.int32)
    tile = jnp.sum((opening[None, :] <= count[:, None]).astype(jnp.int32), axis=1) - 1
    opens = jnp.any(opening[None, :] == count[:, None], axis=1)
    visit = 1 - opens.astype(jnp.int32)
    wanted = jnp.minimum(count - tile - visit, local_rows - 1)
    chosen = (rank[None, :] == wanted[:, None]).astype(jnp.int32)
    table = jnp.stack([serial, offsets[:, 0], offsets[:, 1]])
    picked = jnp.sum(chosen[None] * table[:, None, :], axis=2)
    plan = jnp.concatenate([tile[None], visit[None], picked], 0)
    return jnp.pad(plan, ((0, 0), (0, 1)), constant_values=-1)


def visit_all(plan, column, probe_wave, intensities, tables_of):
    nbatch, slices, _, tile_rows, tile_cols = column.shape
    extent = probe_wave.shape[-1]
    fore, back, prop = tables_of
    steps = plan.shape[1] - 1
    local_rows = intensities.shape[0]
    tile_block = (1, slices, 2, tile_rows, tile_cols)

    def whole(shape):
        return pl.BlockSpec(
            shape, lambda i, plan_ref: (0,) * len(shape), pipeline_mode=pl.Buffered(1)
        )

    return pl.pallas_call(
        visit_kernel,
        out_shape=(
            jax.ShapeDtypeStruct(column.shape, jnp.bfloat16),
            jax.ShapeDtypeStruct((2, extent, extent), jnp.float32),
        ),
        grid_spec=pltpu.PrefetchScalarGridSpec(
            num_scalar_prefetch=1,
            grid=(steps,),
            in_specs=[
                pl.BlockSpec(tile_block, lambda i, plan_ref: (plan_ref[0, i], 0, 0, 0, 0)),
                pl.BlockSpec((1, extent, extent), lambda i, plan_ref: (plan_ref[2, i], 0, 0)),
                whole(probe_wave.shape),
                whole(fore.shape),
                whole(back.shape),
                whole(prop.shape),
            ],
            out_specs=(
                pl.BlockSpec(tile_block, lambda i, plan_ref: (plan_ref[0, i], 0, 0, 0, 0)),
                pl.BlockSpec((2, extent, extent), lambda i, plan_ref: (0, 0, 0)),
            ),
            scratch_shapes=[
                pltpu.VMEM((slices, 2, tile_rows + sublanes, tile_cols), jnp.float32),
                pltpu.VMEM((slices, 2, tile_rows + sublanes, tile_cols), jnp.float32),
                pltpu.VMEM((slices, 2, extent, extent), jnp.float32),
                pltpu.VMEM((slices, 2, extent, extent), jnp.bfloat16),
                pltpu.VMEM((2, extent, extent), jnp.float32),
            ],
        ),
        compiler_params=pltpu.CompilerParams(
            dimension_semantics=("arbitrary",), vmem_limit_bytes=48 * 1024 * 1024
        ),
        cost_estimate=pl.CostEstimate(
            flops=local_rows * (3 * slices) * 16 * extent**3,
            bytes_accessed=2 * column.size * 2 + intensities.size * 4,
            transcendentals=0,
        ),
    )(plan, column, intensities, probe_wave, fore, back, prop)


def tv_local(padded):
    corner_cells = padded[:, :, :-1, :-1]
    down_diff = padded[:, :, 1:, :-1] - corner_cells
    right_diff = padded[:, :, :-1, 1:] - corner_cells
    weight = 1.0 / jnp.sqrt(
        jnp.sum(down_diff * down_diff + right_diff * right_diff, axis=1, keepdims=True) + tv_smooth
    )
    flow_down = weight * down_diff
    flow_right = weight * right_diff
    return (
        flow_down[:, :, :-1, 1:]
        + flow_right[:, :, 1:, :-1]
        - flow_down[:, :, 1:, 1:]
        - flow_right[:, :, 1:, 1:]
    )


def on_device(object_field, probe_wave, intensities, owner_rows, offsets):
    extent = probe_wave.shape[-1]
    nbatch = lax.axis_size("batch")
    column = lax.all_gather(object_field.astype(jnp.bfloat16), "batch", axis=0, tiled=False)
    padded = extended(object_field, (("batch", 2), ("tile", 3)), 1)
    plan = visiting_plan(owner_rows[:, 0], offsets, nbatch)
    cos_table, sin_table, prop_real, prop_imag = tables(extent)
    fore = jnp.concatenate(
        [
            jnp.concatenate([cos_table, -sin_table], 1),
            jnp.concatenate([sin_table, cos_table], 1),
        ],
        0,
    )
    back = jnp.concatenate(
        [
            jnp.concatenate([cos_table, sin_table], 1),
            jnp.concatenate([-sin_table, cos_table], 1),
        ],
        0,
    )
    prop = jnp.stack([prop_real, prop_imag])
    sums, probe_local = visit_all(plan, column, probe_wave, intensities, (fore, back, prop))
    returned = lax.all_to_all(sums, "batch", split_axis=0, concat_axis=0, tiled=True)
    probe_total = lax.psum(probe_local, ("batch", "tile"))
    field_grad = jnp.sum(returned.astype(jnp.float32), axis=0)
    new_object = object_field - update_rate * (field_grad + tv_weight * tv_local(padded))
    new_probe = probe_wave.astype(jnp.float32) - probe_rate * probe_total
    return (new_object, new_probe)


def solution(mesh):
    return jax.shard_map(
        on_device,
        mesh=mesh,
        in_specs=(
            P(None, None, "batch", "tile"),
            P(),
            P(("batch", "tile"), None, None),
            P(("batch", "tile"), None),
            P(("batch", "tile"), None),
        ),
        out_specs=(P(None, None, "batch", "tile"), P()),
        check_vma=False,
    )
```

```python
import math

import jax
import jax.numpy as jnp
from jax import lax
from jax.experimental import pallas as pl
from jax.experimental.pallas import tpu as pltpu
from jax.sharding import PartitionSpec as P

update_rate = 0.1
tv_weight = 12.0
tv_smooth = 1.0
probe_rate = 0.04
sublanes = 8


def extended(x, sides, width):
    for axis, dim in sides:
        size, length = (lax.axis_size(axis), x.shape[dim])
        up = [(i, (i + 1) % size) for i in range(size)]
        down = [(j, i) for i, j in up]
        last = lax.slice_in_dim(x, length - width, length, axis=dim)
        first = lax.slice_in_dim(x, 0, width, axis=dim)
        before = lax.ppermute(last, axis, up)
        after = lax.ppermute(first, axis, down)
        x = jnp.concatenate([before, x, after], axis=dim)
    return x


def tables(extent):
    counter = jnp.arange(extent, dtype=jnp.int32)
    product = counter[:, None] * counter[None, :] % extent
    angles = product.astype(jnp.float32) * (2.0 * math.pi / extent)
    scaling = 1.0 / math.sqrt(extent)
    cos_table = (jnp.cos(angles) * scaling).astype(jnp.bfloat16)
    sin_table = (-jnp.sin(angles) * scaling).astype(jnp.bfloat16)
    frequency = (counter + extent // 2) % extent - extent // 2
    squared = (frequency * frequency).astype(jnp.float32)
    phases = -(0.5 / extent) * (squared[:, None] + squared[None, :])
    return (cos_table, sin_table, jnp.cos(phases), jnp.sin(phases))


def transform(real_part, imag_part, left_table, right_table):
    extent = real_part.shape[0]
    stacked = jnp.concatenate([real_part, imag_part], 0)
    mid = jnp.dot(left_table, stacked, preferred_element_type=jnp.float32).astype(jnp.bfloat16)
    second = jnp.dot(
        jnp.concatenate([mid[:extent], mid[extent:]], 1),
        right_table,
        preferred_element_type=jnp.float32,
    )
    return (second[:, :extent], second[:, extent:])


def visit_kernel(
    plan_ref,
    tile_ref,
    measured_ref,
    probe_ref,
    fore_ref,
    back_ref,
    prop_ref,
    sums_ref,
    total_ref,
    wide,
    summed,
    trans,
    psi,
    total,
):
    step = pl.program_id(0)
    slices = tile_ref.shape[1]
    tile_cols = tile_ref.shape[-1]
    extent = probe_ref.shape[-1]
    last_step = pl.num_programs(0) - 1
    opens = plan_ref[1, step] == 0

    @pl.when(step == 0)
    def _():
        total[...] = jnp.zeros_like(total)

    @pl.when(opens)
    def _():
        wide[:, :, : tile_ref.shape[3], :] = tile_ref[0].astype(jnp.float32)
        summed[...] = jnp.zeros_like(summed)

    @pl.when(jnp.logical_not(opens))
    def _():
        row_at = plan_ref[3, step]
        col_at = plan_ref[4, step]
        back_shift = lax.rem(tile_cols - col_at, tile_cols)
        span = extent + sublanes
        row_rest = lax.rem(row_at, sublanes)
        rows = pl.ds(pl.multiple_of(row_at - row_rest, sublanes), span)
        row_shift = lax.rem(span - row_rest, span)
        fore = fore_ref[...]
        back = back_ref[...]

        def add_grad(slab, part, value):
            value = value.astype(jnp.bfloat16).astype(jnp.float32)
            below = jnp.zeros((sublanes, extent), jnp.float32)
            beside = jnp.zeros((span, tile_cols - extent), jnp.float32)
            value = pltpu.roll(jnp.concatenate([value, below], 0), row_rest, 0)
            placed = pltpu.roll(jnp.concatenate([value, beside], 1), col_at, 1)
            summed[slab, part, rows, :] = summed[slab, part, rows, :] + placed

        for slab in range(slices):
            for part in range(2):
                cut = pltpu.roll(wide[slab, part, rows, :], back_shift, 1)[:, :extent]
                trans[slab, part] = pltpu.roll(cut, row_shift, 0)[:extent]
        psi[0] = probe_ref[...]
        for slab in range(slices):
            wave_real = psi[slab, 0].astype(jnp.float32)
            wave_imag = psi[slab, 1].astype(jnp.float32)
            trans_real = trans[slab, 0]
            trans_imag = trans[slab, 1]
            prod_real = (wave_real * trans_real - wave_imag * trans_imag).astype(jnp.bfloat16)
            prod_imag = (wave_real * trans_imag + wave_imag * trans_real).astype(jnp.bfloat16)
            far_real, far_imag = transform(prod_real, prod_imag, fore, back)
            if slab + 1 < slices:
                prop_real = prop_ref[0]
                prop_imag = prop_ref[1]
                kick_real = (prop_real * far_real - prop_imag * far_imag).astype(jnp.bfloat16)
                kick_imag = (prop_real * far_imag + prop_imag * far_real).astype(jnp.bfloat16)
                near_real, near_imag = transform(kick_real, kick_imag, back, fore)
                psi[slab + 1, 0] = near_real.astype(jnp.bfloat16)
                psi[slab + 1, 1] = near_imag.astype(jnp.bfloat16)
        misfit = 0.5 * (far_real * far_real + far_imag * far_imag - measured_ref[0])
        chi_real = (misfit * far_real).astype(jnp.bfloat16)
        chi_imag = (misfit * far_imag).astype(jnp.bfloat16)
        grad_real, grad_imag = transform(chi_real, chi_imag, back, fore)
        for slab in reversed(range(slices)):
            wave_real = psi[slab, 0].astype(jnp.float32)
            wave_imag = psi[slab, 1].astype(jnp.float32)
            trans_real = trans[slab, 0]
            trans_imag = trans[slab, 1]
            add_grad(slab, 0, grad_real * wave_real + grad_imag * wave_imag)
            add_grad(slab, 1, grad_imag * wave_real - grad_real * wave_imag)
            dpsi_real = grad_real * trans_real + grad_imag * trans_imag
            dpsi_imag = grad_imag * trans_real - grad_real * trans_imag
            if slab > 0:
                back_real, back_imag = transform(
                    dpsi_real.astype(jnp.bfloat16), dpsi_imag.astype(jnp.bfloat16), back, fore
                )
                prop_real = prop_ref[0]
                prop_imag = prop_ref[1]
                turn_real = (prop_real * back_real + prop_imag * back_imag).astype(jnp.bfloat16)
                turn_imag = (prop_real * back_imag - prop_imag * back_real).astype(jnp.bfloat16)
                grad_real, grad_imag = transform(turn_real, turn_imag, fore, back)
        total[0] = total[0] + dpsi_real
        total[1] = total[1] + dpsi_imag

    @pl.when(plan_ref[0, step + 1] != plan_ref[0, step])
    def _():
        sums_ref[0] = summed[:, :, : sums_ref.shape[3], :].astype(jnp.bfloat16)

    @pl.when(step == last_step)
    def _():
        total_ref[...] = total[...]


def visiting_plan(targets, offsets, nbatch):
    local_rows = targets.shape[0]
    steps = local_rows + nbatch
    serial = jnp.arange(local_rows, dtype=jnp.int32)
    ahead = (targets[None, :] < targets[:, None]) | (
        (targets[None, :] == targets[:, None]) & (serial[None, :] < serial[:, None])
    )
    rank = jnp.sum(ahead.astype(jnp.int32), axis=1)
    rows = jnp.arange(nbatch, dtype=jnp.int32)
    opening = rows + jnp.sum((targets[None, :] < rows[:, None]).astype(jnp.int32), axis=1)
    count = jnp.arange(steps, dtype=jnp.int32)
    tile = jnp.sum((opening[None, :] <= count[:, None]).astype(jnp.int32), axis=1) - 1
    opens = jnp.any(opening[None, :] == count[:, None], axis=1)
    visit = 1 - opens.astype(jnp.int32)
    wanted = jnp.minimum(count - tile - visit, local_rows - 1)
    chosen = (rank[None, :] == wanted[:, None]).astype(jnp.int32)
    table = jnp.stack([serial, offsets[:, 0], offsets[:, 1]])
    picked = jnp.sum(chosen[None] * table[:, None, :], axis=2)
    plan = jnp.concatenate([tile[None], visit[None], picked], 0)
    return jnp.pad(plan, ((0, 0), (0, 1)), constant_values=-1)


def visit_all(plan, column, probe_wave, intensities, tables_of):
    nbatch, slices, _, tile_rows, tile_cols = column.shape
    extent = probe_wave.shape[-1]
    fore, back, prop = tables_of
    steps = plan.shape[1] - 1
    local_rows = intensities.shape[0]
    tile_block = (1, slices, 2, tile_rows, tile_cols)

    def whole(shape):
        return pl.BlockSpec(
            shape, lambda i, plan_ref: (0,) * len(shape), pipeline_mode=pl.Buffered(1)
        )

    return pl.pallas_call(
        visit_kernel,
        out_shape=(
            jax.ShapeDtypeStruct(column.shape, jnp.bfloat16),
            jax.ShapeDtypeStruct((2, extent, extent), jnp.float32),
        ),
        grid_spec=pltpu.PrefetchScalarGridSpec(
            num_scalar_prefetch=1,
            grid=(steps,),
            in_specs=[
                pl.BlockSpec(tile_block, lambda i, plan_ref: (plan_ref[0, i], 0, 0, 0, 0)),
                pl.BlockSpec((1, extent, extent), lambda i, plan_ref: (plan_ref[2, i], 0, 0)),
                whole(probe_wave.shape),
                whole(fore.shape),
                whole(back.shape),
                whole(prop.shape),
            ],
            out_specs=(
                pl.BlockSpec(tile_block, lambda i, plan_ref: (plan_ref[0, i], 0, 0, 0, 0)),
                pl.BlockSpec((2, extent, extent), lambda i, plan_ref: (0, 0, 0)),
            ),
            scratch_shapes=[
                pltpu.VMEM((slices, 2, tile_rows + sublanes, tile_cols), jnp.float32),
                pltpu.VMEM((slices, 2, tile_rows + sublanes, tile_cols), jnp.float32),
                pltpu.VMEM((slices, 2, extent, extent), jnp.float32),
                pltpu.VMEM((slices, 2, extent, extent), jnp.bfloat16),
                pltpu.VMEM((2, extent, extent), jnp.float32),
            ],
        ),
        compiler_params=pltpu.CompilerParams(
            dimension_semantics=("arbitrary",),
            vmem_limit_bytes=48 * 1024 * 1024,
        ),
        cost_estimate=pl.CostEstimate(
            flops=local_rows * (3 * slices) * 16 * extent**3,
            bytes_accessed=2 * column.size * 2 + intensities.size * 4,
            transcendentals=0,
        ),
    )(plan, column, intensities, probe_wave, fore, back, prop)


def tv_local(padded):
    corner_cells = padded[:, :, :-1, :-1]
    down_diff = padded[:, :, 1:, :-1] - corner_cells
    right_diff = padded[:, :, :-1, 1:] - corner_cells
    weight = 1.0 / jnp.sqrt(
        jnp.sum(down_diff * down_diff + right_diff * right_diff, axis=1, keepdims=True) + tv_smooth
    )
    flow_down = weight * down_diff
    flow_right = weight * right_diff
    return (
        flow_down[:, :, :-1, 1:]
        + flow_right[:, :, 1:, :-1]
        - flow_down[:, :, 1:, 1:]
        - flow_right[:, :, 1:, 1:]
    )


def on_device(object_field, probe_wave, intensities, owner_rows, offsets):
    extent = probe_wave.shape[-1]
    nbatch = lax.axis_size("batch")
    column = lax.all_gather(object_field.astype(jnp.bfloat16), "batch", axis=0, tiled=False)
    padded = extended(object_field, (("batch", 2), ("tile", 3)), 1)
    plan = visiting_plan(owner_rows[:, 0], offsets, nbatch)
    cos_table, sin_table, prop_real, prop_imag = tables(extent)
    fore = jnp.concatenate(
        [
            jnp.concatenate([cos_table, -sin_table], 1),
            jnp.concatenate([sin_table, cos_table], 1),
        ],
        0,
    )
    back = jnp.concatenate(
        [
            jnp.concatenate([cos_table, sin_table], 1),
            jnp.concatenate([-sin_table, cos_table], 1),
        ],
        0,
    )
    prop = jnp.stack([prop_real, prop_imag])
    smoothing = tv_local(padded)
    column, smoothing = lax.optimization_barrier((column, smoothing))
    sums, probe_local = visit_all(plan, column, probe_wave, intensities, (fore, back, prop))
    everyone = ("batch", "tile")
    devices = nbatch * lax.axis_size("tile")
    shares = lax.all_to_all(
        probe_local.reshape(devices, -1, extent), everyone, split_axis=0, concat_axis=0, tiled=True
    )
    probe_share = jnp.sum(shares, axis=0)
    sums, probe_share = lax.optimization_barrier((sums, probe_share))
    returned = lax.all_to_all(sums, "batch", split_axis=0, concat_axis=0, tiled=True)
    probe_total = lax.all_gather(probe_share, everyone, axis=0, tiled=True)
    probe_total = probe_total.reshape(probe_wave.shape)
    field_grad = jnp.sum(returned.astype(jnp.float32), axis=0)
    new_object = object_field - update_rate * (field_grad + tv_weight * smoothing)
    new_probe = probe_wave.astype(jnp.float32) - probe_rate * probe_total
    return (new_object, new_probe)


def solution(mesh):
    return jax.shard_map(
        on_device,
        mesh=mesh,
        in_specs=(
            P(None, None, "batch", "tile"),
            P(),
            P(("batch", "tile"), None, None),
            P(("batch", "tile"), None),
            P(("batch", "tile"), None),
        ),
        out_specs=(P(None, None, "batch", "tile"), P()),
        check_vma=False,
    )
```
